32 devices in a mesh: dev: 8 (over z, x), ma: 4 (over y, core).
Axes of the slice: x: 2, y: 2, z: 4, core: 2. Of those that a mesh axis runs over, the one named last changes fastest.
Arguments:
- inputs: bfloat16 [8192, 2048], P('ma', 'dev'), may hold values from -6 to 6
- cotangent: bfloat16 [8192, 2048], P('ma', 'dev'), may hold values from -6 to 6
- factors: bfloat16 [4, 64, 16384], P(None, 'ma', 'dev'), may hold values from -0.5 to 0.5
- exponents: int32 [4, 64], P(None, 'ma'), may hold values from -6 to -4
- error_buffer: bfloat16 [8, 4, 64, 16384], P('dev', None, 'ma'), may hold values from -96 to 96
Outputs:
- output: bfloat16 [8192, 2048], P('ma', 'dev')
- input_grad: bfloat16 [8192, 2048], P('ma', 'dev')
- grad_mean: float32 [4, 64, 16384], P(None, 'ma', 'dev')
- new_error: bfloat16 [8, 4, 64, 16384], P('dev', None, 'ma')
The draws below stay inside these ranges and needn't reach their ends.
All inputs are finite; a program needn't handle non-finite values.
Results may differ from the reference program's by a relative error of at most 0.0057.
Values may be sent and summed in bfloat16 or wider, within the bound.
A program may use at most 64 MiB of HBM per device.

```python
import jax
import jax.numpy as jnp
from jax import lax

NB = 64
B = 128
D = 8192
FACTORS = 4
TOK_DEV = 256
GROUPS = 8
TOKENS = 2048


def place_ends(entries, stream_key, low, top_value):
    shape = entries.shape
    index_at = [jax.random.randint(jax.random.fold_in(stream_key, axis), (), 0, shape[axis]) for axis in range(len(shape))]
    entries = entries.at[tuple(index_at)].set(low)
    longest = shape.index(max(shape))
    index_at[longest] = (index_at[longest] + 1) % shape[longest]
    return entries.at[tuple(index_at)].set(top_value)


def level_of(key, shape, shards, least, top_value):
    gain, own = 1.0, jax.random.fold_in(key, 6)
    for dim, shards_of in shards:
        steps = jnp.exp(jax.random.uniform(jax.random.fold_in(own, dim), (shards_of,), jnp.float32, least / len(shards), top_value / len(shards)))
        gain = gain * jnp.repeat(steps, shape[dim] // shards_of).reshape([-1 if axis == dim else 1 for axis in range(len(shape))])
    return gain


def gaussian(stream_key, extent, width, limit, shards=(), kind=jnp.bfloat16):
    array = width * jax.random.normal(stream_key, extent, jnp.float32)
    if shards:
        array = array * level_of(stream_key, extent, shards, -0.22, 0.18)
    return jnp.clip(array, -limit, limit).astype(kind)


def setup_inputs(seed: int = 0) -> dict:
    key_of = jax.random.split(jax.random.key(seed), 6)
    inputs = gaussian(key_of[0], (D, TOKENS), 1.0, 6.0, ((0, 4), (1, 8)))
    cotangent = gaussian(key_of[1], (D, TOKENS), 1.0, 6.0, ((0, 4), (1, 8)))
    factors = gaussian(key_of[2], (FACTORS, NB, B * B), B ** -0.5, 0.5, ((1, 4), (2, 8)))
    exponents = place_ends(jax.random.randint(key_of[3], (FACTORS, NB), -6, -3), jax.random.fold_in(key_of[3], 1), -6, (-3) - 1).astype(jnp.int32)
    error_buffer = gaussian(key_of[4], (GROUPS, FACTORS, NB, B * B), 16.0, 96.0, ((0, 8), (2, 4)))
    return {"inputs": inputs, "cotangent": cotangent, "factors": factors, "exponents": exponents, "error_buffer": error_buffer}


code_limit = 127.0

def permute(values):
    tok_count = values.shape[-1]
    grouped = values.reshape(NB, B // NB, NB, tok_count)
    return jnp.transpose(grouped, (2, 1, 0, 3)).reshape(NB, B, tok_count)

def block_forward(weights, values):
    return jnp.einsum('ncd,nct->ndt', weights.astype(jnp.float32), values.astype(jnp.float32))

def block_backward(weights, values):
    return jnp.einsum('ncd,ndt->nct', weights.astype(jnp.float32), values.astype(jnp.float32))

def outer_sum(left, right):
    return jnp.einsum('nct,ndt->ncd', left.astype(jnp.float32), right.astype(jnp.float32))

def reference(inputs, cotangent, factors, exponents, error_buffer):
    matrices = factors.reshape(FACTORS, NB, B, B)
    scale_inverse = jnp.left_shift(jnp.ones_like(exponents), -exponents).astype(jnp.float32)[:, :, None]

    def split_groups(whole):
        return jnp.transpose(whole.reshape(NB, B, GROUPS, TOK_DEV), (2, 0, 1, 3))

    def join_groups(parts):
        return jnp.transpose(parts, (1, 2, 0, 3)).reshape(NB * B, GROUPS * TOK_DEV)

    def one_group(code_total, group_items):
        block_in, block_cot, error_part = group_items
        first_out = block_forward(matrices[0], block_in).astype(jnp.bfloat16)
        mixed_one = permute(first_out)
        second_out = block_forward(matrices[1], mixed_one).astype(jnp.bfloat16)
        pre_gelu = permute(second_out)
        hidden_wide, gelu_back = jax.vjp(jax.nn.gelu, pre_gelu.astype(jnp.float32))
        hidden = hidden_wide.astype(jnp.bfloat16)
        third_out = block_forward(matrices[2], hidden).astype(jnp.bfloat16)
        mixed_two = permute(third_out)
        fourth_out = block_forward(matrices[3], mixed_two).astype(jnp.bfloat16)
        output_part = (block_in.astype(jnp.float32) + permute(fourth_out).astype(jnp.float32)).astype(jnp.bfloat16)
        back_four = permute(block_cot)
        d_mixed_two = block_backward(matrices[3], back_four).astype(jnp.bfloat16)
        d_third = permute(d_mixed_two)
        d_pre = gelu_back(block_backward(matrices[2], d_third))[0].astype(jnp.bfloat16)
        d_second = permute(d_pre)
        d_mixed_one = block_backward(matrices[1], d_second).astype(jnp.bfloat16)
        d_first = permute(d_mixed_one)
        grad_part = (block_cot.astype(jnp.float32) + block_backward(matrices[0], d_first)).astype(jnp.bfloat16)
        gradients = jnp.stack([outer_sum(block_in, d_first), outer_sum(mixed_one, d_second), outer_sum(hidden, d_third), outer_sum(mixed_two, back_four)]).reshape(FACTORS, NB, B * B)
        totals = gradients + error_part.astype(jnp.float32)
        code_values = jnp.clip(totals * scale_inverse, -code_limit, code_limit)
        new_part = (totals - code_values / scale_inverse).astype(jnp.bfloat16)
        return (code_total + code_values, (output_part, grad_part, new_part))
    code_total, stacked = lax.scan(one_group, jnp.zeros((FACTORS, NB, B * B), jnp.float32), (split_groups(inputs), split_groups(cotangent), error_buffer))
    grad_mean = code_total / scale_inverse / GROUPS
    return (join_groups(stacked[0]), join_groups(stacked[1]), grad_mean, stacked[2])
```

```python
import functools

import jax
import jax.numpy as jnp
from jax import lax
from jax.experimental import pallas as pl
from jax.experimental.pallas import tpu as pltpu
from jax.sharding import PartitionSpec as P

B = 128
LANES = 128
LIMIT = 127.0
C0 = 0.7978845608028654
C1 = 0.044715
F32 = jnp.float32
BF16 = jnp.bfloat16
ORDER = (0, 3, 1, 2)
COT, ONE, DTHIRD, PRE, DSECOND, TWO, DFIRST, LAST = range(8)


def dot(a, b):
    return lax.dot_general(a, b, (((1,), (0,)), ((), ())), preferred_element_type=F32)


def dot_nt(a, b):
    return lax.dot_general(a, b, (((1,), (1,)), ((), ())), preferred_element_type=F32)


def kernel(
    G, M, inp, cot, fac, expo, err, out, igrad, gmean, nerr,
    x_v, c_v, e_v, hid, rx, tx, sf, gs, wg, w_n, w_t, cod, crx, o_v, g_v, m_v, n_v,
    ld, st, xs, xr, ws, wr, cs_s, cs_r,
):
    F, nb, S = fac.shape
    H = x_v.shape[0]
    NBT = M * nb
    U = B // NBT
    CS = S // B
    seg = nb * U * nb
    ma = lax.axis_index("ma")
    dev = lax.axis_index("dev")

    def lanes(h):
        return slice(h * LANES, (h + 1) * LANES)

    loads = []
    for h in range(H):
        loads.append(pltpu.make_async_copy(cot.at[:, lanes(h)], c_v.at[h], ld.at[h]))
    for h in range(H):
        loads.append(pltpu.make_async_copy(inp.at[:, lanes(h)], x_v.at[h], ld.at[H + h]))
    loads.append(pltpu.make_async_copy(err.at[0], e_v, ld.at[2 * H]))
    own = pltpu.make_async_copy(fac, wg.at[:, dev], ld.at[2 * H + 1])
    for cp in loads:
        cp.start()
    own.start()

    barrier = pltpu.get_barrier_semaphore()
    for d in range(1, M):
        pl.semaphore_signal(barrier, inc=1, device_id={"ma": lax.rem(ma + d, M)}, device_id_type=pl.DeviceIdType.MESH)

    def greet(d, _):
        pl.semaphore_signal(barrier, inc=1, device_id={"dev": lax.rem(dev + d, G)}, device_id_type=pl.DeviceIdType.MESH)
        return 0

    lax.fori_loop(1, G, greet, 0)

    def w_copy(f, d, slot):
        return pltpu.make_async_remote_copy(
            src_ref=fac.at[f], dst_ref=wg.at[f, slot], send_sem=ws.at[f, d], recv_sem=wr.at[f, d],
            device_id={"dev": lax.rem(dev + d, G)}, device_id_type=pl.DeviceIdType.MESH,
        )

    def x_copy(k, h, d, src):
        return pltpu.make_async_remote_copy(
            src_ref=tx.at[k, h, d - 1], dst_ref=rx.at[k, h, :, pl.ds(pl.multiple_of(src * nb, nb), nb), :],
            send_sem=xs.at[k, h, d], recv_sem=xr.at[k, h, d],
            device_id={"ma": lax.rem(ma + d, M)}, device_id_type=pl.DeviceIdType.MESH,
        )

    def c_copy(f, d, slot):
        return pltpu.make_async_remote_copy(
            src_ref=cod.at[f, d], dst_ref=crx.at[f, slot], send_sem=cs_s.at[f, d], recv_sem=cs_r.at[f, d],
            device_id={"dev": lax.rem(dev + d, G)}, device_id_type=pl.DeviceIdType.MESH,
        )

    def spread(i, value):
        for u in range(U):
            sf[pl.ds(u * nb + i, NBT, stride=U * nb), :] = value[u * NBT:(u + 1) * NBT]

    def part(m):
        rows = sf[pl.ds(pl.multiple_of(m * seg, seg), seg), :]
        return rows.astype(BF16).reshape(nb * U, nb, LANES)

    def pack(k, h):
        for d in range(1, M):
            tx[k, h, d - 1] = part(lax.rem(ma + d, M))

    def launch(k, h):
        for d in range(1, M):
            x_copy(k, h, d, ma).start()

    def keep(k, h):
        rx[k, h, :, pl.ds(pl.multiple_of(ma * nb, nb), nb), :] = part(ma)

    def send(k, h):
        for d in range(1, M):
            tx[k, h, d - 1] = part(lax.rem(ma + d, M))
            x_copy(k, h, d, ma).start()
        keep(k, h)

    def arrive(k, h):
        for d in range(1, M):
            x_copy(k, h, d, lax.rem(ma + M - d, M)).wait_recv()

    def block(k, h, i):
        return rx[k, h, pl.ds(i * U, U)].reshape(B, LANES)

    def rows_of(ref, h, i):
        return ref[h, pl.ds(pl.multiple_of(i * B, B), B), :]

    def each(fn, unroll=4):
        def step(i, _):
            fn(i)
            return 0

        lax.fori_loop(0, nb, step, 0, unroll=unroll)

    def weights(f):
        def arrived(d, _):
            w_copy(f, d, lax.rem(dev + G - d, G)).wait_recv()
            return 0

        lax.fori_loop(1, G, arrived, 0)

        def widen(g, _):
            for c in range(CS):
                at = pl.multiple_of((g * CS + c) * nb, nb)
                gs[pl.ds(at, nb), :] = wg[f, g, :, c * B:(c + 1) * B].astype(F32)
            return 0

        lax.fori_loop(0, G, widen, 0)

        def take(n):
            w = gs[pl.ds(n, B, stride=nb), :]
            w_n[f, n] = w.astype(BF16)
            w_t[f, n] = w.T.astype(BF16)

        each(take, 2)

    def gradient(f, left, right):
        def one(n):
            total = dot_nt(left(0, n), right(0, n))
            for h in range(1, H):
                total = total + dot_nt(left(h, n), right(h, n))
            gs[pl.ds(n, B, stride=nb), :] = total

        each(one)
        row = lax.broadcasted_iota(jnp.int32, (nb, B), 0)
        power = jnp.zeros((nb, B), jnp.int32)
        for n in range(nb):
            power = jnp.where(row == n, expo[f, n], power)
        scale = jnp.left_shift(jnp.ones_like(power), -power).astype(F32)
        inverse = jnp.left_shift(jnp.ones_like(power), 24 + power).astype(F32) * (2.0 ** -24)

        def quantize(g, put):
            for c in range(CS):
                col = pl.ds(pl.multiple_of((g * CS + c) * B, B), B)
                total = gs[pl.ds(pl.multiple_of((g * CS + c) * nb, nb), nb), :] + e_v[f, :, col].astype(F32)
                code = jnp.clip(total * scale, -LIMIT, LIMIT)
                n_v[f, :, col] = (total - code * inverse).astype(BF16)
                put(c, code.astype(BF16))

        def away(d, _):
            def put(c, code):
                cod[f, d, :, c * B:(c + 1) * B] = code

            quantize(lax.rem(dev + d, G), put)
            c_copy(f, d, dev).start()
            return 0

        lax.fori_loop(1, G, away, 0)

        def put_own(c, code):
            crx[f, dev, :, c * B:(c + 1) * B] = code

        quantize(dev, put_own)
        pltpu.make_async_copy(n_v.at[f], nerr.at[0, f], st.at[f]).start()
        return inverse

    def spread_cot(h):
        each(lambda i: spread(i, rows_of(c_v, h, i).astype(F32)))

    loads[0].wait()
    spread_cot(0)
    pack(COT, 0)
    keep(COT, 0)
    pl.semaphore_wait(barrier, M - 1 + G - 1)
    launch(COT, 0)
    for f in ORDER:
        def push(d, _, f=f):
            w_copy(f, d, dev).start()
            return 0

        lax.fori_loop(1, G, push, 0)
    for h in range(1, H):
        loads[h].wait()
        spread_cot(h)
        send(COT, h)

    own.wait()
    for h in range(H):
        loads[H + h].wait()
    weights(0)
    for h in range(H):
        each(lambda i: spread(i, dot(w_t[0, i], rows_of(x_v, h, i))))
        send(ONE, h)
    weights(3)
    for h in range(H):
        arrive(COT, h)
        each(lambda i: spread(i, dot(w_n[3, i], block(COT, h, i))))
        send(DTHIRD, h)
    weights(1)
    for h in range(H):
        arrive(ONE, h)
        each(lambda i: spread(i, dot(w_t[1, i], block(ONE, h, i))))
        send(PRE, h)
    weights(2)
    for h in range(H):
        arrive(DTHIRD, h)
    for h in range(H):
        arrive(PRE, h)

        def middle(i):
            v = block(PRE, h, i).astype(F32)
            square = v * v
            t = jnp.tanh(C0 * (v + C1 * (square * v)))
            half = 0.5 * (1.0 + t)
            hid[h, pl.ds(pl.multiple_of(i * B, B), B), :] = (v * half).astype(BF16)
            slope = half + 0.5 * v * (1.0 - t * t) * (C0 * (1.0 + 3.0 * C1 * square))
            spread(i, dot(w_n[2, i], block(DTHIRD, h, i)) * slope)

        each(middle, 2)
        send(DSECOND, h)
    for h in range(H):
        each(lambda i: spread(i, dot(w_t[2, i], rows_of(hid, h, i))))
        send(TWO, h)
    loads[2 * H].wait()
    inverses = {}
    inverses[2] = gradient(2, lambda h, n: rows_of(hid, h, n), lambda h, n: block(DTHIRD, h, n))
    for h in range(H):
        arrive(DSECOND, h)
        each(lambda i: spread(i, dot(w_n[1, i], block(DSECOND, h, i))))
        send(DFIRST, h)
    inverses[1] = gradient(1, lambda h, n: block(ONE, h, n), lambda h, n: block(DSECOND, h, n))
    for h in range(H):
        arrive(TWO, h)
        each(lambda i: spread(i, dot(w_t[3, i], block(TWO, h, i))))
        send(LAST, h)
    inverses[3] = gradient(3, lambda h, n: block(TWO, h, n), lambda h, n: block(COT, h, n))
    for h in range(H):
        arrive(DFIRST, h)
    inverses[0] = gradient(0, lambda h, n: rows_of(x_v, h, n), lambda h, n: block(DFIRST, h, n))
    stores = []
    for h in range(H):
        def back(i):
            value = rows_of(c_v, h, i).astype(F32) + dot(w_n[0, i], block(DFIRST, h, i))
            g_v[h, pl.ds(pl.multiple_of(i * B, B), B), :] = value.astype(BF16)

        each(back)
        stores.append(pltpu.make_async_copy(g_v.at[h], igrad.at[:, lanes(h)], st.at[2 * F + h]))
        stores[-1].start()

    def mean(f):
        def arrived(d, _):
            c_copy(f, d, lax.rem(dev + G - d, G)).wait_recv()
            return 0

        lax.fori_loop(1, G, arrived, 0)

        def column(c, _):
            col = pl.ds(pl.multiple_of(c * B, B), B)
            total = crx[f, 0, :, col].astype(F32)
            for g in range(1, G):
                total = total + crx[f, g, :, col].astype(F32)
            m_v[f, :, col] = total * inverses[f] / G
            return 0

        lax.fori_loop(0, CS, column, 0)
        stores.append(pltpu.make_async_copy(m_v.at[f], gmean.at[f], st.at[F + f]))
        stores[-1].start()

    for f in (2, 1, 3):
        mean(f)
    for h in range(H):
        arrive(LAST, h)

        def finish(i):
            value = rows_of(x_v, h, i).astype(F32) + block(LAST, h, i).astype(F32)
            o_v[h, pl.ds(pl.multiple_of(i * B, B), B), :] = value.astype(BF16)

        each(finish)
        stores.append(pltpu.make_async_copy(o_v.at[h], out.at[:, lanes(h)], st.at[2 * F + H + h]))
        stores[-1].start()
    mean(0)
    for f in range(F):
        pltpu.make_async_copy(n_v.at[f], nerr.at[0, f], st.at[f]).wait()
    for cp in stores:
        cp.wait()

    def sent(d, _):
        for f in range(F):
            w_copy(f, d, dev).wait_send()
            c_copy(f, d, dev).wait_send()
        return 0

    lax.fori_loop(1, G, sent, 0)
    for k in range(8):
        for h in range(H):
            for d in range(1, M):
                x_copy(k, h, d, ma).wait_send()


def step(G, M, inp, cot, fac, expo, err):
    F, nb, S = fac.shape
    R, T = inp.shape
    H = T // LANES
    NBT = M * nb
    U = B // NBT
    hbm = pl.BlockSpec(memory_space=pl.ANY)
    return pl.pallas_call(
        functools.partial(kernel, G, M),
        out_shape=(
            jax.ShapeDtypeStruct((R, T), BF16),
            jax.ShapeDtypeStruct((R, T), BF16),
            jax.ShapeDtypeStruct(fac.shape, F32),
            jax.ShapeDtypeStruct(err.shape, BF16),
        ),
        in_specs=[hbm, hbm, hbm, pl.BlockSpec(memory_space=pltpu.SMEM), hbm],
        out_specs=(hbm,) * 4,
        scratch_shapes=[
            pltpu.VMEM((H, R, LANES), BF16),
            pltpu.VMEM((H, R, LANES), BF16),
            pltpu.VMEM((F, nb, B * B), BF16),
            pltpu.VMEM((H, R, LANES), BF16),
            pltpu.VMEM((8, H, nb * U, NBT, LANES), BF16),
            pltpu.VMEM((8, H, M - 1, nb * U, nb, LANES), BF16),
            pltpu.VMEM((R, LANES), F32),
            pltpu.VMEM((R, LANES), F32),
            pltpu.VMEM((F, G, nb, S), BF16),
            pltpu.VMEM((F, nb, B, B), BF16),
            pltpu.VMEM((F, nb, B, B), BF16),
            pltpu.VMEM((F, G, nb, S), BF16),
            pltpu.VMEM((F, G, nb, S), BF16),
            pltpu.VMEM((H, R, LANES), BF16),
            pltpu.VMEM((H, R, LANES), BF16),
            pltpu.VMEM((F, nb, S), F32),
            pltpu.VMEM((F, nb, B * B), BF16),
            pltpu.SemaphoreType.DMA((2 * H + 2,)),
            pltpu.SemaphoreType.DMA((2 * F + 2 * H,)),
            pltpu.SemaphoreType.DMA((8, H, M)),
            pltpu.SemaphoreType.DMA((8, H, M)),
            pltpu.SemaphoreType.DMA((F, G)),
            pltpu.SemaphoreType.DMA((F, G)),
            pltpu.SemaphoreType.DMA((F, G)),
            pltpu.SemaphoreType.DMA((F, G)),
        ],
        compiler_params=pltpu.CompilerParams(
            collective_id=0, has_side_effects=True, vmem_limit_bytes=60 * 1024 * 1024
        ),
    )(inp, cot, fac, expo, err)


def solution(mesh):
    G, M = mesh.shape["dev"], mesh.shape["ma"]
    in_specs = (
        P("ma", "dev"),
        P("ma", "dev"),
        P(None, "ma", "dev"),
        P(None, "ma"),
        P("dev", None, "ma", None),
    )
    out_specs = (P("ma", "dev"), P("ma", "dev"), P(None, "ma", "dev"), P("dev", None, "ma", None))
    return jax.shard_map(
        functools.partial(step, G, M), mesh=mesh, in_specs=in_specs, out_specs=out_specs, check_vma=False
    )
```

```python
import functools

import jax
import jax.numpy as jnp
from jax import lax
from jax.experimental import pallas as pl
from jax.experimental.pallas import tpu as pltpu
from jax.sharding import PartitionSpec as P

B = 128
LANES = 128
LIMIT = 127.0
C0 = 0.7978845608028654
C1 = 0.044715
F32 = jnp.float32
BF16 = jnp.bfloat16
ORDER = (0, 3, 1, 2)
COT, ONE, DTHIRD, PRE, DSECOND, TWO, DFIRST, LAST = range(8)


def dot(a, b):
    return lax.dot_general(a, b, (((1,), (0,)), ((), ())), preferred_element_type=F32)


def dot_nt(a, b):
    return lax.dot_general(a, b, (((1,), (1,)), ((), ())), preferred_element_type=F32)


def kernel(
    G, M, inp, cot, fac, expo, err, out, igrad, gmean, nerr,
    x_v, c_v, e_v, hid, rx, tx, sf, gs, wg, w_n, w_t, cod, crx, o_v, g_v, m_v, n_v,
    ld, st, xs, xr, ws, wr, ps, pr, cs_s, cs_r,
):
    F, nb, S = fac.shape
    H = x_v.shape[0]
    NBT = M * nb
    U = B // NBT
    CS = S // B
    seg = nb * U * nb
    ma = lax.axis_index("ma")
    dev = lax.axis_index("dev")
    half_group = G // 2
    partner = dev + 1 - 2 * lax.rem(dev, 2)

    def lanes(h):
        return slice(h * LANES, (h + 1) * LANES)

    loads = []
    for h in range(H):
        loads.append(pltpu.make_async_copy(cot.at[:, lanes(h)], c_v.at[h], ld.at[h]))
    for h in range(H):
        loads.append(pltpu.make_async_copy(inp.at[:, lanes(h)], x_v.at[h], ld.at[H + h]))
    loads.append(pltpu.make_async_copy(err.at[0], e_v, ld.at[2 * H]))
    own = pltpu.make_async_copy(fac, wg.at[:, dev], ld.at[2 * H + 1])
    for cp in loads:
        cp.start()
    own.start()

    barrier = pltpu.get_barrier_semaphore()
    for d in range(1, M):
        pl.semaphore_signal(barrier, inc=1, device_id={"ma": lax.rem(ma + d, M)}, device_id_type=pl.DeviceIdType.MESH)

    def greet(d, _):
        pl.semaphore_signal(barrier, inc=1, device_id={"dev": lax.rem(dev + d, G)}, device_id_type=pl.DeviceIdType.MESH)
        return 0

    lax.fori_loop(1, G, greet, 0)

    def w_copy(f, d, slot):
        return pltpu.make_async_remote_copy(
            src_ref=fac.at[f], dst_ref=wg.at[f, slot], send_sem=ws.at[f, d], recv_sem=wr.at[f, d],
            device_id={"dev": lax.rem(dev + 2 * d, G)}, device_id_type=pl.DeviceIdType.MESH,
        )

    def p_copy(f, d, source, slot):
        return pltpu.make_async_remote_copy(
            src_ref=source, dst_ref=wg.at[f, slot], send_sem=ps.at[f, d], recv_sem=pr.at[f, d],
            device_id={"dev": partner}, device_id_type=pl.DeviceIdType.MESH,
        )

    def forward(f):
        def one(d, _):
            slot = lax.rem(dev + G - 2 * d, G)
            w_copy(f, d, slot).wait_recv()
            p_copy(f, d, wg.at[f, slot], slot).start()
            return 0

        lax.fori_loop(1, half_group, one, 0)

    def x_copy(k, h, d, src):
        return pltpu.make_async_remote_copy(
            src_ref=tx.at[k, h, d - 1], dst_ref=rx.at[k, h, :, pl.ds(pl.multiple_of(src * nb, nb), nb), :],
            send_sem=xs.at[k, h, d], recv_sem=xr.at[k, h, d],
            device_id={"ma": lax.rem(ma + d, M)}, device_id_type=pl.DeviceIdType.MESH,
        )

    def c_copy(f, d, slot):
        return pltpu.make_async_remote_copy(
            src_ref=cod.at[f, d], dst_ref=crx.at[f, slot], send_sem=cs_s.at[f, d], recv_sem=cs_r.at[f, d],
            device_id={"dev": lax.rem(dev + d, G)}, device_id_type=pl.DeviceIdType.MESH,
        )

    def spread(i, value):
        for u in range(U):
            sf[pl.ds(u * nb + i, NBT, stride=U * nb), :] = value[u * NBT:(u + 1) * NBT]

    def part(m):
        rows = sf[pl.ds(pl.multiple_of(m * seg, seg), seg), :]
        return rows.astype(BF16).reshape(nb * U, nb, LANES)

    def pack(k, h):
        for d in range(1, M):
            tx[k, h, d - 1] = part(lax.rem(ma + d, M))

    def launch(k, h):
        for d in range(1, M):
            x_copy(k, h, d, ma).start()

    def keep(k, h):
        rx[k, h, :, pl.ds(pl.multiple_of(ma * nb, nb), nb), :] = part(ma)

    def send(k, h):
        for d in range(1, M):
            tx[k, h, d - 1] = part(lax.rem(ma + d, M))
            x_copy(k, h, d, ma).start()
        keep(k, h)

    def arrive(k, h):
        for d in range(1, M):
            x_copy(k, h, d, lax.rem(ma + M - d, M)).wait_recv()

    def block(k, h, i):
        return rx[k, h, pl.ds(i * U, U)].reshape(B, LANES)

    def rows_of(ref, h, i):
        return ref[h, pl.ds(pl.multiple_of(i * B, B), B), :]

    def each(fn, unroll=4):
        def step(i, _):
            fn(i)
            return 0

        lax.fori_loop(0, nb, step, 0, unroll=unroll)

    def weights(f):
        def arrived(d, _):
            slot = lax.rem(partner + G - 2 * d, G)
            p_copy(f, d, wg.at[f, slot], slot).wait_recv()
            return 0

        lax.fori_loop(0, half_group, arrived, 0)

        def widen(g, _):
            for c in range(CS):
                at = pl.multiple_of((g * CS + c) * nb, nb)
                gs[pl.ds(at, nb), :] = wg[f, g, :, c * B:(c + 1) * B].astype(F32)
            return 0

        lax.fori_loop(0, G, widen, 0)

        def take(n):
            w = gs[pl.ds(n, B, stride=nb), :]
            w_n[f, n] = w.astype(BF16)
            w_t[f, n] = w.T.astype(BF16)

        each(take, 2)

    def gradient(f, left, right):
        def one(n):
            total = dot_nt(left(0, n), right(0, n))
            for h in range(1, H):
                total = total + dot_nt(left(h, n), right(h, n))
            gs[pl.ds(n, B, stride=nb), :] = total

        each(one)
        row = lax.broadcasted_iota(jnp.int32, (nb, B), 0)
        power = jnp.zeros((nb, B), jnp.int32)
        for n in range(nb):
            power = jnp.where(row == n, expo[f, n], power)
        scale = jnp.left_shift(jnp.ones_like(power), -power).astype(F32)
        inverse = jnp.left_shift(jnp.ones_like(power), 24 + power).astype(F32) * (2.0 ** -24)

        def quantize(g, put):
            for c in range(CS):
                col = pl.ds(pl.multiple_of((g * CS + c) * B, B), B)
                total = gs[pl.ds(pl.multiple_of((g * CS + c) * nb, nb), nb), :] + e_v[f, :, col].astype(F32)
                code = jnp.clip(total * scale, -LIMIT, LIMIT)
                n_v[f, :, col] = (total - code * inverse).astype(BF16)
                put(c, code.astype(BF16))

        def away(d, _):
            def put(c, code):
                cod[f, d, :, c * B:(c + 1) * B] = code

            quantize(lax.rem(dev + d, G), put)
            c_copy(f, d, dev).start()
            return 0

        lax.fori_loop(1, G, away, 0)

        def put_own(c, code):
            crx[f, dev, :, c * B:(c + 1) * B] = code

        quantize(dev, put_own)
        pltpu.make_async_copy(n_v.at[f], nerr.at[0, f], st.at[f]).start()
        return inverse

    def spread_cot(h):
        each(lambda i: spread(i, rows_of(c_v, h, i).astype(F32)))

    loads[0].wait()
    spread_cot(0)
    pack(COT, 0)
    keep(COT, 0)
    pl.semaphore_wait(barrier, M - 1 + G - 1)
    launch(COT, 0)
    for f in ORDER:
        def push(d, _, f=f):
            w_copy(f, d, dev).start()
            return 0

        lax.fori_loop(1, half_group, push, 0)
        p_copy(f, 0, fac.at[f], dev).start()
    for h in range(1, H):
        loads[h].wait()
        spread_cot(h)
        send(COT, h)

    own.wait()
    for h in range(H):
        loads[H + h].wait()
    forward(0)
    weights(0)
    for h in range(H):
        each(lambda i: spread(i, dot(w_t[0, i], rows_of(x_v, h, i))))
        send(ONE, h)
        if h == 0:
            forward(3)
    weights(3)
    for h in range(H):
        arrive(COT, h)
        each(lambda i: spread(i, dot(w_n[3, i], block(COT, h, i))))
        send(DTHIRD, h)
        if h == 0:
            forward(1)
    weights(1)
    for h in range(H):
        arrive(ONE, h)
        each(lambda i: spread(i, dot(w_t[1, i], block(ONE, h, i))))
        send(PRE, h)
        if h == 0:
            forward(2)
    weights(2)
    for h in range(H):
        arrive(DTHIRD, h)
    for h in range(H):
        arrive(PRE, h)

        def middle(i):
            v = block(PRE, h, i).astype(F32)
            square = v * v
            t = jnp.tanh(C0 * (v + C1 * (square * v)))
            half = 0.5 * (1.0 + t)
            hid[h, pl.ds(pl.multiple_of(i * B, B), B), :] = (v * half).astype(BF16)
            slope = half + 0.5 * v * (1.0 - t * t) * (C0 * (1.0 + 3.0 * C1 * square))
            spread(i, dot(w_n[2, i], block(DTHIRD, h, i)) * slope)

        each(middle, 2)
        send(DSECOND, h)
    for h in range(H):
        each(lambda i: spread(i, dot(w_t[2, i], rows_of(hid, h, i))))
        send(TWO, h)
    loads[2 * H].wait()
    inverses = {}
    inverses[2] = gradient(2, lambda h, n: rows_of(hid, h, n), lambda h, n: block(DTHIRD, h, n))
    for h in range(H):
        arrive(DSECOND, h)
        each(lambda i: spread(i, dot(w_n[1, i], block(DSECOND, h, i))))
        send(DFIRST, h)
    inverses[1] = gradient(1, lambda h, n: block(ONE, h, n), lambda h, n: block(DSECOND, h, n))
    for h in range(H):
        arrive(TWO, h)
        each(lambda i: spread(i, dot(w_t[3, i], block(TWO, h, i))))
        send(LAST, h)
    inverses[3] = gradient(3, lambda h, n: block(TWO, h, n), lambda h, n: block(COT, h, n))
    for h in range(H):
        arrive(DFIRST, h)
    inverses[0] = gradient(0, lambda h, n: rows_of(x_v, h, n), lambda h, n: block(DFIRST, h, n))
    stores = []
    for h in range(H):
        def back(i):
            value = rows_of(c_v, h, i).astype(F32) + dot(w_n[0, i], block(DFIRST, h, i))
            g_v[h, pl.ds(pl.multiple_of(i * B, B), B), :] = value.astype(BF16)

        each(back)
        stores.append(pltpu.make_async_copy(g_v.at[h], igrad.at[:, lanes(h)], st.at[2 * F + h]))
        stores[-1].start()

    def mean(f):
        def arrived(d, _):
            c_copy(f, d, lax.rem(dev + G - d, G)).wait_recv()
            return 0

        lax.fori_loop(1, G, arrived, 0)

        def column(c, _):
            col = pl.ds(pl.multiple_of(c * B, B), B)
            total = crx[f, 0, :, col].astype(F32)
            for g in range(1, G):
                total = total + crx[f, g, :, col].astype(F32)
            m_v[f, :, col] = total * inverses[f] / G
            return 0

        lax.fori_loop(0, CS, column, 0)
        stores.append(pltpu.make_async_copy(m_v.at[f], gmean.at[f], st.at[F + f]))
        stores[-1].start()

    for f in (2, 1, 3):
        mean(f)
    for h in range(H):
        arrive(LAST, h)

        def finish(i):
            value = rows_of(x_v, h, i).astype(F32) + block(LAST, h, i).astype(F32)
            o_v[h, pl.ds(pl.multiple_of(i * B, B), B), :] = value.astype(BF16)

        each(finish)
        stores.append(pltpu.make_async_copy(o_v.at[h], out.at[:, lanes(h)], st.at[2 * F + H + h]))
        stores[-1].start()
    mean(0)
    for f in range(F):
        pltpu.make_async_copy(n_v.at[f], nerr.at[0, f], st.at[f]).wait()
    for cp in stores:
        cp.wait()

    def sent(d, _):
        for f in range(F):
            c_copy(f, d, dev).wait_send()
        return 0

    lax.fori_loop(1, G, sent, 0)

    def handed(d, _):
        for f in range(F):
            w_copy(f, d, dev).wait_send()
            slot = lax.rem(dev + G - 2 * d, G)
            p_copy(f, d, wg.at[f, slot], slot).wait_send()
        return 0

    lax.fori_loop(1, half_group, handed, 0)
    for f in range(F):
        p_copy(f, 0, fac.at[f], dev).wait_send()
    for k in range(8):
        for h in range(H):
            for d in range(1, M):
                x_copy(k, h, d, ma).wait_send()


def step(G, M, inp, cot, fac, expo, err):
    F, nb, S = fac.shape
    R, T = inp.shape
    H = T // LANES
    NBT = M * nb
    U = B // NBT
    hbm = pl.BlockSpec(memory_space=pl.ANY)
    return pl.pallas_call(
        functools.partial(kernel, G, M),
        out_shape=(
            jax.ShapeDtypeStruct((R, T), BF16),
            jax.ShapeDtypeStruct((R, T), BF16),
            jax.ShapeDtypeStruct(fac.shape, F32),
            jax.ShapeDtypeStruct(err.shape, BF16),
        ),
        in_specs=[hbm, hbm, hbm, pl.BlockSpec(memory_space=pltpu.SMEM), hbm],
        out_specs=(hbm,) * 4,
        scratch_shapes=[
            pltpu.VMEM((H, R, LANES), BF16),
            pltpu.VMEM((H, R, LANES), BF16),
            pltpu.VMEM((F, nb, B * B), BF16),
            pltpu.VMEM((H, R, LANES), BF16),
            pltpu.VMEM((8, H, nb * U, NBT, LANES), BF16),
            pltpu.VMEM((8, H, M - 1, nb * U, nb, LANES), BF16),
            pltpu.VMEM((R, LANES), F32),
            pltpu.VMEM((R, LANES), F32),
            pltpu.VMEM((F, G, nb, S), BF16),
            pltpu.VMEM((F, nb, B, B), BF16),
            pltpu.VMEM((F, nb, B, B), BF16),
            pltpu.VMEM((F, G, nb, S), BF16),
            pltpu.VMEM((F, G, nb, S), BF16),
            pltpu.VMEM((H, R, LANES), BF16),
            pltpu.VMEM((H, R, LANES), BF16),
            pltpu.VMEM((F, nb, S), F32),
            pltpu.VMEM((F, nb, B * B), BF16),
            pltpu.SemaphoreType.DMA((2 * H + 2,)),
            pltpu.SemaphoreType.DMA((2 * F + 2 * H,)),
            pltpu.SemaphoreType.DMA((8, H, M)),
            pltpu.SemaphoreType.DMA((8, H, M)),
            pltpu.SemaphoreType.DMA((F, G // 2)),
            pltpu.SemaphoreType.DMA((F, G // 2)),
            pltpu.SemaphoreType.DMA((F, G // 2)),
            pltpu.SemaphoreType.DMA((F, G // 2)),
            pltpu.SemaphoreType.DMA((F, G)),
            pltpu.SemaphoreType.DMA((F, G)),
        ],
        compiler_params=pltpu.CompilerParams(
            collective_id=0, has_side_effects=True, vmem_limit_bytes=60 * 1024 * 1024
        ),
    )(inp, cot, fac, expo, err)


def solution(mesh):
    G, M = mesh.shape["dev"], mesh.shape["ma"]
    in_specs = (
        P("ma", "dev"),
        P("ma", "dev"),
        P(None, "ma", "dev"),
        P(None, "ma"),
        P("dev", None, "ma", None),
    )
    out_specs = (P("ma", "dev"), P("ma", "dev"), P(None, "ma", "dev"), P("dev", None, "ma", None))
    return jax.shard_map(
        functools.partial(step, G, M), mesh=mesh, in_specs=in_specs, out_specs=out_specs, check_vma=False
    )
```

```python
import functools

import jax
import jax.numpy as jnp
from jax import lax
from jax.experimental import pallas as pl
from jax.experimental.pallas import tpu as pltpu
from jax.sharding import PartitionSpec as P

B = 128
LANES = 128
LIMIT = 127.0
C0 = 0.7978845608028654
C1 = 0.044715
F32 = jnp.float32
BF16 = jnp.bfloat16
ORDER = (0, 3, 1, 2)
COT, ONE, DTHIRD, PRE, DSECOND, TWO, DFIRST, LAST = range(8)


def dot(a, b):
    return lax.dot_general(a, b, (((1,), (0,)), ((), ())), preferred_element_type=F32)


def dot_nt(a, b):
    return lax.dot_general(a, b, (((1,), (1,)), ((), ())), preferred_element_type=F32)


def kernel(
    G, M, inp, cot, fac, expo, err, out, igrad, gmean, nerr,
    x_v, c_v, e_v, hid, rx, tx, sf, gs, wg, w_n, w_t, cod, crx, o_v, g_v, m_v, n_v,
    ld, st, xs, xr, ws, wr, ps, pr, cs_s, cs_r, qs, qr,
):
    F, nb, S = fac.shape
    H = x_v.shape[0]
    NBT = M * nb
    U = B // NBT
    CS = S // B
    seg = nb * U * nb
    ma = lax.axis_index("ma")
    dev = lax.axis_index("dev")
    half_group = G // 2
    partner = dev + 1 - 2 * lax.rem(dev, 2)

    def lanes(h):
        return slice(h * LANES, (h + 1) * LANES)

    loads = []
    for h in range(H):
        loads.append(pltpu.make_async_copy(cot.at[:, lanes(h)], c_v.at[h], ld.at[h]))
    for h in range(H):
        loads.append(pltpu.make_async_copy(inp.at[:, lanes(h)], x_v.at[h], ld.at[H + h]))
    loads.append(pltpu.make_async_copy(err.at[0], e_v, ld.at[2 * H]))
    own = pltpu.make_async_copy(fac, wg.at[:, dev], ld.at[2 * H + 1])
    for cp in loads:
        cp.start()
    own.start()

    barrier = pltpu.get_barrier_semaphore()
    for d in range(1, M):
        pl.semaphore_signal(barrier, inc=1, device_id={"ma": lax.rem(ma + d, M)}, device_id_type=pl.DeviceIdType.MESH)

    def greet(d, _):
        pl.semaphore_signal(barrier, inc=1, device_id={"dev": lax.rem(dev + d, G)}, device_id_type=pl.DeviceIdType.MESH)
        return 0

    lax.fori_loop(1, G, greet, 0)

    def w_copy(f, d, slot):
        return pltpu.make_async_remote_copy(
            src_ref=fac.at[f], dst_ref=wg.at[f, slot], send_sem=ws.at[f, d], recv_sem=wr.at[f, d],
            device_id={"dev": lax.rem(dev + 2 * d, G)}, device_id_type=pl.DeviceIdType.MESH,
        )

    def p_copy(f, d, source, slot):
        return pltpu.make_async_remote_copy(
            src_ref=source, dst_ref=wg.at[f, slot], send_sem=ps.at[f, d], recv_sem=pr.at[f, d],
            device_id={"dev": partner}, device_id_type=pl.DeviceIdType.MESH,
        )

    def forward(f):
        def one(d, _):
            slot = lax.rem(dev + G - 2 * d, G)
            w_copy(f, d, slot).wait_recv()
            p_copy(f, d, wg.at[f, slot], slot).start()
            return 0

        lax.fori_loop(1, half_group, one, 0)

    def x_copy(k, h, d, src):
        return pltpu.make_async_remote_copy(
            src_ref=tx.at[k, h, d - 1], dst_ref=rx.at[k, h, :, pl.ds(pl.multiple_of(src * nb, nb), nb), :],
            send_sem=xs.at[k, h, d], recv_sem=xr.at[k, h, d],
            device_id={"ma": lax.rem(ma + d, M)}, device_id_type=pl.DeviceIdType.MESH,
        )

    def q_copy(f, d):
        return pltpu.make_async_remote_copy(
            src_ref=cod.at[f, d], dst_ref=crx.at[f, half_group + d], send_sem=qs.at[f, d], recv_sem=qr.at[f, d],
            device_id={"dev": partner}, device_id_type=pl.DeviceIdType.MESH,
        )

    def c_copy(f, d):
        return pltpu.make_async_remote_copy(
            src_ref=cod.at[f, half_group + d], dst_ref=crx.at[f, d], send_sem=cs_s.at[f, d], recv_sem=cs_r.at[f, d],
            device_id={"dev": lax.rem(dev + 2 * d, G)}, device_id_type=pl.DeviceIdType.MESH,
        )

    def combine(f):
        def one(d, _):
            q_copy(f, d).wait_recv()
            both = cod[f, half_group + d].astype(F32) + crx[f, half_group + d].astype(F32)
            cod[f, half_group + d] = both.astype(BF16)
            c_copy(f, d).start()
            return 0

        lax.fori_loop(1, half_group, one, 0)
        q_copy(f, 0).wait_recv()
        crx[f, 0] = (cod[f, half_group].astype(F32) + crx[f, half_group].astype(F32)).astype(BF16)

    def spread(i, value):
        for u in range(U):
            sf[pl.ds(u * nb + i, NBT, stride=U * nb), :] = value[u * NBT:(u + 1) * NBT]

    def part(m):
        rows = sf[pl.ds(pl.multiple_of(m * seg, seg), seg), :]
        return rows.astype(BF16).reshape(nb * U, nb, LANES)

    def pack(k, h):
        for d in range(1, M):
            tx[k, h, d - 1] = part(lax.rem(ma + d, M))

    def launch(k, h):
        for d in range(1, M):
            x_copy(k, h, d, ma).start()

    def keep(k, h):
        rx[k, h, :, pl.ds(pl.multiple_of(ma * nb, nb), nb), :] = part(ma)

    def send(k, h):
        for d in range(1, M):
            tx[k, h, d - 1] = part(lax.rem(ma + d, M))
            x_copy(k, h, d, ma).start()
        keep(k, h)

    def arrive(k, h):
        for d in range(1, M):
            x_copy(k, h, d, lax.rem(ma + M - d, M)).wait_recv()

    def block(k, h, i):
        return rx[k, h, pl.ds(i * U, U)].reshape(B, LANES)

    def rows_of(ref, h, i):
        return ref[h, pl.ds(pl.multiple_of(i * B, B), B), :]

    def each(fn, unroll=4):
        def step(i, _):
            fn(i)
            return 0

        lax.fori_loop(0, nb, step, 0, unroll=unroll)

    def weights(f):
        def arrived(d, _):
            slot = lax.rem(partner + G - 2 * d, G)
            p_copy(f, d, wg.at[f, slot], slot).wait_recv()
            return 0

        lax.fori_loop(0, half_group, arrived, 0)

        def widen(g, _):
            for c in range(CS):
                at = pl.multiple_of((g * CS + c) * nb, nb)
                gs[pl.ds(at, nb), :] = wg[f, g, :, c * B:(c + 1) * B].astype(F32)
            return 0

        lax.fori_loop(0, G, widen, 0)

        def take(n):
            w = gs[pl.ds(n, B, stride=nb), :]
            w_n[f, n] = w.astype(BF16)
            w_t[f, n] = w.T.astype(BF16)

        each(take, 2)

    def gradient(f, left, right):
        def one(n):
            total = dot_nt(left(0, n), right(0, n))
            for h in range(1, H):
                total = total + dot_nt(left(h, n), right(h, n))
            gs[pl.ds(n, B, stride=nb), :] = total

        each(one)
        row = lax.broadcasted_iota(jnp.int32, (nb, B), 0)
        power = jnp.zeros((nb, B), jnp.int32)
        for n in range(nb):
            power = jnp.where(row == n, expo[f, n], power)
        scale = jnp.left_shift(jnp.ones_like(power), -power).astype(F32)
        inverse = jnp.left_shift(jnp.ones_like(power), 24 + power).astype(F32) * (2.0 ** -24)

        def quantize(g, put):
            for c in range(CS):
                col = pl.ds(pl.multiple_of((g * CS + c) * B, B), B)
                total = gs[pl.ds(pl.multiple_of((g * CS + c) * nb, nb), nb), :] + e_v[f, :, col].astype(F32)
                code = jnp.clip(total * scale, -LIMIT, LIMIT)
                n_v[f, :, col] = (total - code * inverse).astype(BF16)
                put(c, code.astype(BF16))

        def put(slot):
            def store(c, code):
                cod[f, slot, :, c * B:(c + 1) * B] = code

            return store

        def away(step, _):
            d = lax.rem(step + 1, half_group)
            quantize(lax.rem(partner + 2 * d, G), put(d))
            q_copy(f, d).start()
            return 0

        lax.fori_loop(0, half_group, away, 0)

        def stay(d, _):
            quantize(lax.rem(dev + 2 * d, G), put(half_group + d))
            return 0

        lax.fori_loop(0, half_group, stay, 0)
        pltpu.make_async_copy(n_v.at[f], nerr.at[0, f], st.at[f]).start()
        return inverse

    def spread_cot(h):
        each(lambda i: spread(i, rows_of(c_v, h, i).astype(F32)))

    loads[0].wait()
    spread_cot(0)
    pack(COT, 0)
    keep(COT, 0)
    pl.semaphore_wait(barrier, M - 1 + G - 1)
    launch(COT, 0)
    for f in ORDER:
        def push(d, _, f=f):
            w_copy(f, d, dev).start()
            return 0

        lax.fori_loop(1, half_group, push, 0)
        p_copy(f, 0, fac.at[f], dev).start()
    for h in range(1, H):
        loads[h].wait()
        spread_cot(h)
        send(COT, h)

    own.wait()
    for h in range(H):
        loads[H + h].wait()
    forward(0)
    weights(0)
    for h in range(H):
        each(lambda i: spread(i, dot(w_t[0, i], rows_of(x_v, h, i))))
        send(ONE, h)
        if h == 0:
            forward(3)
    weights(3)
    for h in range(H):
        arrive(COT, h)
        each(lambda i: spread(i, dot(w_n[3, i], block(COT, h, i))))
        send(DTHIRD, h)
        if h == 0:
            forward(1)
    weights(1)
    for h in range(H):
        arrive(ONE, h)
        each(lambda i: spread(i, dot(w_t[1, i], block(ONE, h, i))))
        send(PRE, h)
        if h == 0:
            forward(2)
    weights(2)
    for h in range(H):
        arrive(DTHIRD, h)
    for h in range(H):
        arrive(PRE, h)

        def middle(i):
            v = block(PRE, h, i).astype(F32)
            square = v * v
            t = jnp.tanh(C0 * (v + C1 * (square * v)))
            half = 0.5 * (1.0 + t)
            hid[h, pl.ds(pl.multiple_of(i * B, B), B), :] = (v * half).astype(BF16)
            slope = half + 0.5 * v * (1.0 - t * t) * (C0 * (1.0 + 3.0 * C1 * square))
            spread(i, dot(w_n[2, i], block(DTHIRD, h, i)) * slope)

        each(middle, 2)
        send(DSECOND, h)
    for h in range(H):
        each(lambda i: spread(i, dot(w_t[2, i], rows_of(hid, h, i))))
        send(TWO, h)
    loads[2 * H].wait()
    inverses = {}
    inverses[2] = gradient(2, lambda h, n: rows_of(hid, h, n), lambda h, n: block(DTHIRD, h, n))
    for h in range(H):
        arrive(DSECOND, h)
        each(lambda i: spread(i, dot(w_n[1, i], block(DSECOND, h, i))))
        send(DFIRST, h)
    combine(2)
    inverses[1] = gradient(1, lambda h, n: block(ONE, h, n), lambda h, n: block(DSECOND, h, n))
    for h in range(H):
        arrive(TWO, h)
        each(lambda i: spread(i, dot(w_t[3, i], block(TWO, h, i))))
        send(LAST, h)
    combine(1)
    inverses[3] = gradient(3, lambda h, n: block(TWO, h, n), lambda h, n: block(COT, h, n))
    combine(3)
    for h in range(H):
        arrive(DFIRST, h)
    inverses[0] = gradient(0, lambda h, n: rows_of(x_v, h, n), lambda h, n: block(DFIRST, h, n))
    combine(0)
    stores = []
    for h in range(H):
        def back(i):
            value = rows_of(c_v, h, i).astype(F32) + dot(w_n[0, i], block(DFIRST, h, i))
            g_v[h, pl.ds(pl.multiple_of(i * B, B), B), :] = value.astype(BF16)

        each(back)
        stores.append(pltpu.make_async_copy(g_v.at[h], igrad.at[:, lanes(h)], st.at[2 * F + h]))
        stores[-1].start()

    def mean(f):
        def arrived(d, _):
            c_copy(f, d).wait_recv()
            return 0

        lax.fori_loop(1, half_group, arrived, 0)

        def column(c, _):
            col = pl.ds(pl.multiple_of(c * B, B), B)
            total = crx[f, 0, :, col].astype(F32)
            for g in range(1, half_group):
                total = total + crx[f, g, :, col].astype(F32)
            m_v[f, :, col] = total * inverses[f] / G
            return 0

        lax.fori_loop(0, CS, column, 0)
        stores.append(pltpu.make_async_copy(m_v.at[f], gmean.at[f], st.at[F + f]))
        stores[-1].start()

    for f in (2, 1, 3):
        mean(f)
    for h in range(H):
        arrive(LAST, h)

        def finish(i):
            value = rows_of(x_v, h, i).astype(F32) + block(LAST, h, i).astype(F32)
            o_v[h, pl.ds(pl.multiple_of(i * B, B), B), :] = value.astype(BF16)

        each(finish)
        stores.append(pltpu.make_async_copy(o_v.at[h], out.at[:, lanes(h)], st.at[2 * F + H + h]))
        stores[-1].start()
    mean(0)
    for f in range(F):
        pltpu.make_async_copy(n_v.at[f], nerr.at[0, f], st.at[f]).wait()
    for cp in stores:
        cp.wait()

    def handed(d, _):
        for f in range(F):
            w_copy(f, d, dev).wait_send()
            q_copy(f, d).wait_send()
            c_copy(f, d).wait_send()
            slot = lax.rem(dev + G - 2 * d, G)
            p_copy(f, d, wg.at[f, slot], slot).wait_send()
        return 0

    lax.fori_loop(1, half_group, handed, 0)
    for f in range(F):
        p_copy(f, 0, fac.at[f], dev).wait_send()
        q_copy(f, 0).wait_send()
    for k in range(8):
        for h in range(H):
            for d in range(1, M):
                x_copy(k, h, d, ma).wait_send()


def step(G, M, inp, cot, fac, expo, err):
    F, nb, S = fac.shape
    R, T = inp.shape
    H = T // LANES
    NBT = M * nb
    U = B // NBT
    hbm = pl.BlockSpec(memory_space=pl.ANY)
    return pl.pallas_call(
        functools.partial(kernel, G, M),
        out_shape=(
            jax.ShapeDtypeStruct((R, T), BF16),
            jax.ShapeDtypeStruct((R, T), BF16),
            jax.ShapeDtypeStruct(fac.shape, F32),
            jax.ShapeDtypeStruct(err.shape, BF16),
        ),
        in_specs=[hbm, hbm, hbm, pl.BlockSpec(memory_space=pltpu.SMEM), hbm],
        out_specs=(hbm,) * 4,
        scratch_shapes=[
            pltpu.VMEM((H, R, LANES), BF16),
            pltpu.VMEM((H, R, LANES), BF16),
            pltpu.VMEM((F, nb, B * B), BF16),
            pltpu.VMEM((H, R, LANES), BF16),
            pltpu.VMEM((8, H, nb * U, NBT, LANES), BF16),
            pltpu.VMEM((8, H, M - 1, nb * U, nb, LANES), BF16),
            pltpu.VMEM((R, LANES), F32),
            pltpu.VMEM((R, LANES), F32),
            pltpu.VMEM((F, G, nb, S), BF16),
            pltpu.VMEM((F, nb, B, B), BF16),
            pltpu.VMEM((F, nb, B, B), BF16),
            pltpu.VMEM((F, G, nb, S), BF16),
            pltpu.VMEM((F, G, nb, S), BF16),
            pltpu.VMEM((H, R, LANES), BF16),
            pltpu.VMEM((H, R, LANES), BF16),
            pltpu.VMEM((F, nb, S), F32),
            pltpu.VMEM((F, nb, B * B), BF16),
            pltpu.SemaphoreType.DMA((2 * H + 2,)),
            pltpu.SemaphoreType.DMA((2 * F + 2 * H,)),
            pltpu.SemaphoreType.DMA((8, H, M)),
            pltpu.SemaphoreType.DMA((8, H, M)),
            pltpu.SemaphoreType.DMA((F, G // 2)),
            pltpu.SemaphoreType.DMA((F, G // 2)),
            pltpu.SemaphoreType.DMA((F, G // 2)),
            pltpu.SemaphoreType.DMA((F, G // 2)),
            pltpu.SemaphoreType.DMA((F, G // 2)),
            pltpu.SemaphoreType.DMA((F, G // 2)),
            pltpu.SemaphoreType.DMA((F, G // 2)),
            pltpu.SemaphoreType.DMA((F, G // 2)),
        ],
        compiler_params=pltpu.CompilerParams(
            collective_id=0, has_side_effects=True, vmem_limit_bytes=60 * 1024 * 1024
        ),
    )(inp, cot, fac, expo, err)


def solution(mesh):
    G, M = mesh.shape["dev"], mesh.shape["ma"]
    in_specs = (
        P("ma", "dev"),
        P("ma", "dev"),
        P(None, "ma", "dev"),
        P(None, "ma"),
        P("dev", None, "ma", None),
    )
    out_specs = (P("ma", "dev"), P("ma", "dev"), P(None, "ma", "dev"), P("dev", None, "ma", None))
    return jax.shard_map(
        functools.partial(step, G, M), mesh=mesh, in_specs=in_specs, out_specs=out_specs, check_vma=False
    )
```
